32 devices in a mesh: dp: 8 (over z, y), expert: 4 (over x, core).
Axes of the slice: x: 2, y: 2, z: 4, core: 2. Of those that a mesh axis runs over, the one named last changes fastest.
Arguments:
- tokens: bfloat16 [4096, 2048], P(('dp', 'expert')), may hold values from -6 to 6
- routes: int32 [4096, 8], P(('dp', 'expert')), may hold values from 0 to 15, all different within a row; in each aligned block of 128 rows (0 to 127, 128 to 255, ...) at most 80 rows name the same one
- gates: bfloat16 [4096, 8], P(('dp', 'expert')), may hold values from 0.099609375 to 0.5
- cotangent: bfloat16 [4096, 2048], P(('dp', 'expert')), may hold values from -6 to 6
- w_gate: bfloat16 [16, 2048, 384], P('dp'), may hold values from -0.125 to 0.125
- w_up: bfloat16 [16, 2048, 384], P('dp'), may hold values from -0.125 to 0.125
- w_down: bfloat16 [16, 384, 2048], P('dp'), may hold values from -0.3125 to 0.3125
Outputs:
- layer_out: bfloat16 [4096, 2048], P(('dp', 'expert'))
- grad_tokens: bfloat16 [4096, 2048], P(('dp', 'expert'))
- grad_gate: bfloat16 [16, 2048, 384], P('dp', 'expert')
- grad_up: bfloat16 [16, 2048, 384], P('dp', 'expert')
- grad_down: bfloat16 [16, 384, 2048], P('dp', None, 'expert')
The draws below stay inside these ranges and needn't reach their ends.
Inputs may be any that keep to these rules, and one draw needn't show every extreme that they name: `routes`: each row names 8 different experts. Among the rows of one device, no expert is named by more than 80 rows, and in every draw some device has an expert named by exactly 80 rows.
All inputs are finite; a program needn't handle non-finite values.
Results may differ from the reference program's by a relative error of at most 0.012.
Values may be sent and summed in bfloat16 or wider, within the bound.
A program may use at most 128 MiB of HBM per device.

```python
import math
import jax
import jax.numpy as jnp
import numpy as np
from jax import lax

D = 2048
F = 384
TOP = 8
TOK_DEV = 128
EXPERTS = 16
CAP = 80
TOKENS = 4096
N_DP = 8
N_EXPERT = 4
DEVICES = 32


def level_of(own_key, extent, shards, least, top_value):
    factor_of = 1.0
    for dim, shards_of in shards:
        steps = jax.random.uniform(jax.random.fold_in(jax.random.fold_in(own_key, 6), dim), (shards_of,), jnp.float32, least / len(shards), top_value / len(shards))
        factor_of = factor_of * jnp.repeat(jnp.exp(steps), extent[dim] // shards_of).reshape((-1,) + (1,) * (len(extent) - 1 - dim))
    return factor_of


def shared_out(own_key, own, number, rows, number_of, top, reach, slope):
    order = jax.random.permutation(own_key, number_of)
    packed, ordinary = shares(number_of, rows * top, reach, slope, True), shares(number_of, rows * top, reach, slope, False)
    places = jnp.arange(number_of)

    def named(tallies, rotation):
        used = int((tallies > 0).sum())
        fixed = max(1, used // 4)
        moved = fixed + (places - fixed + rotation * (used - fixed)) % max(1, number_of - fixed)
        return jnp.zeros((number_of,), jnp.int32).at[order[jnp.where(places < fixed, places, moved)]].set(jnp.asarray(tallies, jnp.int32))

    tallies = jnp.where(number % 4 == 0, named(packed, number // 4), named(ordinary, number - number // 4 - 1))
    mixed = jax.random.permutation(jax.random.fold_in(own, 3), number_of)
    giver, receiver = mixed[0:number_of // 2 * 2:2], mixed[1:number_of // 2 * 2:2]
    slack = jnp.minimum(tallies[giver] - 1, reach - tallies[receiver]) // 2
    slack = jnp.where((giver == order[0]) | (receiver == order[0]) | (tallies[receiver] == 0), 0, jnp.maximum(slack, 0))
    moved = jax.random.randint(jax.random.fold_in(own, 4), (number_of // 2,), 0, 1 << 20) % (slack + 1)
    tallies = tallies.at[giver].add(-moved).at[receiver].add(moved)
    items = jnp.searchsorted(jnp.cumsum(tallies), jnp.arange(rows * top), side="right").astype(jnp.int32)
    grid = items.reshape(top, rows).T
    grid = grid[jax.random.permutation(jax.random.fold_in(own, 1), rows)]
    rotation = jax.random.randint(jax.random.fold_in(own, 2), (rows, 1), 0, top)
    return jnp.take_along_axis(grid, (jnp.arange(top)[None, :] + rotation) % top, axis=1)


def shares(number_of, total, reach, lean, full):
    portions = [(1 << 20) // math.isqrt(standing ** lean) + 1 for standing in range(1, number_of + 1)]
    largest = reach if full else min(reach, max(-(-total // number_of), total * portions[0] // sum(portions)))
    least = 1 if total - largest >= number_of - 1 else 0
    given, rest = [largest] + [least] * (number_of - 1), total - largest - least * (number_of - 1)
    while rest > 0:
        free = [i for i in range(1, number_of) if given[i] < largest] or [i for i in range(1, number_of) if given[i] < reach]
        whole, budget = sum([portions[i] for i in free]), rest
        for i in free:
            more = min(reach - given[i], max(1, budget * portions[i] // whole), rest)
            given[i] = given[i] + more
            rest = rest - more
    return np.array(given)


def bell_draw(rng, extent, scale, most, pieces=(), kind=jnp.bfloat16):
    values = scale * jax.random.normal(rng, extent, jnp.float32)
    if pieces:
        values = values * level_of(rng, extent, pieces, -0.22, 0.18)
    return jnp.clip(values, -most, most).astype(kind)


def setup_inputs(seed: int = 0) -> dict:
    streams_of = jax.random.split(jax.random.key(seed), 8)
    tokens = bell_draw(streams_of[0], (TOKENS, D), 1.0, 6.0, ((0, 32),))
    routes_keys = jax.random.split(jax.random.fold_in(streams_of[1], 1), TOKENS // TOK_DEV)
    routes_turns = jax.random.permutation(jax.random.fold_in(streams_of[1], 3), TOKENS // TOK_DEV)
    routes = jax.vmap(lambda own, number: shared_out(jax.random.fold_in(streams_of[1], 2), own, number, TOK_DEV, EXPERTS, TOP, CAP, 2))(routes_keys, routes_turns).reshape((TOKENS, TOP))
    gates = jnp.clip(0.099609375 + 0.40039062 * jax.random.uniform(streams_of[2], (TOKENS, TOP), jnp.float32) ** level_of(streams_of[2], (TOKENS, TOP), ((0, 32),), -0.2, 0.2), 0.099609375, 0.5).astype(jnp.bfloat16)
    cotangent = bell_draw(streams_of[3], (TOKENS, D), 1.0, 6.0, ((0, 32),))
    w_gate = bell_draw(streams_of[4], (EXPERTS, D, F), D ** -0.5, 0.125, ((0, 8),))
    w_up = bell_draw(streams_of[5], (EXPERTS, D, F), D ** -0.5, 0.125, ((0, 8),))
    w_down = bell_draw(streams_of[6], (EXPERTS, F, D), F ** -0.5, 0.3125, ((0, 8),))
    return {"tokens": tokens, "routes": routes, "gates": gates, "cotangent": cotangent, "w_gate": w_gate, "w_up": w_up, "w_down": w_down}


def expert_pass(x_rows, cot_rows, row_gain, wg, wu, wd):
    gate_act = jnp.dot(x_rows, wg, preferred_element_type=jnp.float32)
    up_act = jnp.dot(x_rows, wu, preferred_element_type=jnp.float32)
    sigma_gate = jax.nn.sigmoid(gate_act)
    smooth = gate_act * sigma_gate
    hidden = (smooth * up_act).astype(jnp.bfloat16)
    result = jnp.dot(hidden, wd, preferred_element_type=jnp.float32).astype(jnp.bfloat16)
    row_cot = (row_gain.astype(jnp.float32)[:, None] * cot_rows.astype(jnp.float32)).astype(jnp.bfloat16)
    grad_hidden = jnp.dot(row_cot, wd.T, preferred_element_type=jnp.float32)
    grad_upact = (grad_hidden * smooth).astype(jnp.bfloat16)
    grad_gateact = (grad_hidden * up_act * sigma_gate * (1.0 + gate_act * (1.0 - sigma_gate))).astype(jnp.bfloat16)
    row_grad = (jnp.dot(grad_gateact, wg.T, preferred_element_type=jnp.float32)
                + jnp.dot(grad_upact, wu.T, preferred_element_type=jnp.float32)).astype(jnp.bfloat16)
    x_group = x_rows.astype(jnp.float32).reshape(N_DP, N_EXPERT, CAP, -1)
    gg_group = grad_gateact.astype(jnp.float32).reshape(N_DP, N_EXPERT, CAP, -1)
    gu_group = grad_upact.astype(jnp.float32).reshape(N_DP, N_EXPERT, CAP, -1)
    hid_group = hidden.astype(jnp.float32).reshape(N_DP, N_EXPERT, CAP, -1)
    cot_group = row_cot.astype(jnp.float32).reshape(N_DP, N_EXPERT, CAP, -1)
    part_g = jnp.einsum("ajcd,ajcf->jdf", x_group, gg_group).astype(jnp.bfloat16)
    part_u = jnp.einsum("ajcd,ajcf->jdf", x_group, gu_group).astype(jnp.bfloat16)
    part_d = jnp.einsum("ajcf,ajcd->jfd", hid_group, cot_group).astype(jnp.bfloat16)
    grad_g = jnp.sum(part_g.astype(jnp.float32), axis=0).astype(jnp.bfloat16)
    grad_u = jnp.sum(part_u.astype(jnp.float32), axis=0).astype(jnp.bfloat16)
    grad_d = jnp.sum(part_d.astype(jnp.float32), axis=0).astype(jnp.bfloat16)
    return result, row_grad, grad_g, grad_u, grad_d


def reference(tokens, routes, gates, cotangent, w_gate, w_up, w_down):
    chosen = routes.reshape(DEVICES, TOK_DEV * TOP)
    columns = jnp.arange(EXPERTS, dtype=jnp.int32)
    onehot = (chosen[:, :, None] == columns[None, None, :]).astype(jnp.int32)
    before = jnp.cumsum(onehot, axis=1) - onehot
    order_in = jnp.sum(before * onehot, axis=2).astype(jnp.int32)
    device_ids = jnp.arange(DEVICES, dtype=jnp.int32)[:, None]
    position = (chosen * (DEVICES * CAP) + device_ids * CAP + order_in).reshape(-1).astype(jnp.int32)
    owner_of = jnp.repeat(jnp.arange(TOKENS, dtype=jnp.int32), TOP)
    total_slots = EXPERTS * DEVICES * CAP
    table = jnp.full((total_slots,), TOKENS, jnp.int32).at[position].set(owner_of)
    table = table.reshape(EXPERTS, DEVICES * CAP)
    gains = jnp.zeros((total_slots,), gates.dtype).at[position].set(gates.reshape(-1))
    gains = gains.reshape(EXPERTS, DEVICES * CAP)
    padded_x = jnp.concatenate([tokens, jnp.zeros((1, D), tokens.dtype)], axis=0)
    padded_c = jnp.concatenate([cotangent, jnp.zeros((1, D), cotangent.dtype)], axis=0)

    def expert_step(carry, inputs):
        out_sum, grad_sum = carry
        row_ids, row_gain, wg, wu, wd = inputs
        result, row_grad, grad_g, grad_u, grad_d = expert_pass(
            padded_x[row_ids], padded_c[row_ids], row_gain, wg, wu, wd)
        out_sum = out_sum.at[row_ids].add(
            row_gain.astype(jnp.float32)[:, None] * result.astype(jnp.float32), mode="drop")
        grad_sum = grad_sum.at[row_ids].add(row_grad.astype(jnp.float32), mode="drop")
        return (out_sum, grad_sum), (grad_g, grad_u, grad_d)

    start = (jnp.zeros((TOKENS, D), jnp.float32), jnp.zeros((TOKENS, D), jnp.float32))
    (out_sum, grad_sum), (grad_gate, grad_up, grad_down) = lax.scan(
        expert_step, start, (table, gains, w_gate, w_up, w_down))
    return (out_sum.astype(jnp.bfloat16), grad_sum.astype(jnp.bfloat16), grad_gate, grad_up, grad_down)
```

```python
import jax
import jax.numpy as jnp
from jax import lax
from jax.sharding import PartitionSpec as P


def expert_forward(arrived, w_gate, w_up, w_down):
    gate_act = jnp.einsum("erd,edf->erf", arrived, w_gate, preferred_element_type=jnp.float32)
    up_act = jnp.einsum("erd,edf->erf", arrived, w_up, preferred_element_type=jnp.float32)
    sigma_gate = jax.nn.sigmoid(gate_act)
    smooth = gate_act * sigma_gate
    hidden = (smooth * up_act).astype(jnp.bfloat16)
    result = jnp.einsum("erf,efd->erd", hidden, w_down, preferred_element_type=jnp.float32).astype(
        jnp.bfloat16
    )
    return (gate_act, up_act, sigma_gate, smooth, hidden, result)


def body(tokens, routes, gates, cotangent, w_gate, w_up, w_down):
    tok_rows, top_k = routes.shape
    width = tokens.shape[1]
    owners = lax.axis_size("dp")
    me = lax.axis_index("dp")
    per_owner = w_gate.shape[0]
    hidden_units = w_gate.shape[2]
    experts = owners * per_owner
    capacity = max(2, tok_rows * top_k * 5 // (4 * experts))
    rows_per_expert = owners * capacity
    both = jnp.concatenate([tokens, cotangent], axis=1)
    all_both = lax.all_gather(both, "dp", axis=0, tiled=True)
    all_routes = lax.all_gather(routes, "dp", axis=0, tiled=True)
    all_gates = lax.all_gather(gates, "dp", axis=0, tiled=True)
    all_x = all_both[:, :width]
    all_c = all_both[:, width:]
    mine = me * per_owner + jnp.arange(per_owner, dtype=jnp.int32)
    hit = all_routes[None, :, :] == mine[:, None, None]
    named = jnp.any(hit, axis=2).astype(jnp.int32)
    gain = jnp.sum(jnp.where(hit, all_gates[None, :, :].astype(jnp.float32), 0.0), axis=2)
    position = jnp.where(named > 0, jnp.cumsum(named, axis=1) - 1, -1)
    pick = position[:, None, :] == jnp.arange(rows_per_expert, dtype=jnp.int32)[None, :, None]
    pick_x = pick.astype(jnp.bfloat16)
    pick_g = jnp.where(pick, gain[:, None, :], 0.0).astype(jnp.bfloat16)
    arrived = jnp.einsum("ept,td->epd", pick_x, all_x, preferred_element_type=jnp.float32).astype(
        jnp.bfloat16
    )
    arrived_grad = jnp.einsum(
        "ept,td->epd", pick_g, all_c, preferred_element_type=jnp.float32
    ).astype(jnp.bfloat16)
    state = expert_forward(arrived, w_gate, w_up, w_down)
    gate_act, up_act, sigma_gate, smooth, hidden, result = state
    out_part = jnp.einsum("ept,epd->td", pick_g, result, preferred_element_type=jnp.float32).astype(
        jnp.bfloat16
    )
    layer_out = lax.psum_scatter(out_part, "dp", scatter_dimension=0, tiled=True)
    grad_hidden = jnp.einsum(
        "erd,efd->erf", arrived_grad, w_down, preferred_element_type=jnp.float32
    )
    grad_upact = (grad_hidden * smooth).astype(jnp.bfloat16)
    grad_gateact = (
        grad_hidden * up_act * sigma_gate * (1.0 + gate_act * (1.0 - sigma_gate))
    ).astype(jnp.bfloat16)
    row_grads = (
        jnp.einsum("erf,edf->erd", grad_gateact, w_gate, preferred_element_type=jnp.float32)
        + jnp.einsum("erf,edf->erd", grad_upact, w_up, preferred_element_type=jnp.float32)
    ).astype(jnp.bfloat16)
    grad_part = jnp.einsum(
        "ept,epd->td", pick_x, row_grads, preferred_element_type=jnp.float32
    ).astype(jnp.bfloat16)
    grad_tokens = lax.psum_scatter(grad_part, "dp", scatter_dimension=0, tiled=True)
    both_factors = jnp.concatenate([grad_gateact, grad_upact], axis=2)
    input_term = jnp.einsum(
        "erd,erf->def", arrived, both_factors, preferred_element_type=jnp.float32
    )
    down_term = jnp.einsum("erf,erd->def", hidden, arrived_grad, preferred_element_type=jnp.float32)
    totals = lax.psum_scatter(
        jnp.concatenate([input_term, down_term], axis=2).astype(jnp.bfloat16),
        "expert",
        scatter_dimension=0,
        tiled=True,
    ).astype(jnp.float32)
    grad_gate = jnp.transpose(totals[:, :, :hidden_units], (1, 0, 2)).astype(jnp.bfloat16)
    grad_up = jnp.transpose(totals[:, :, hidden_units : 2 * hidden_units], (1, 0, 2)).astype(
        jnp.bfloat16
    )
    grad_down = jnp.transpose(totals[:, :, 2 * hidden_units :], (1, 2, 0)).astype(jnp.bfloat16)
    return (layer_out, grad_tokens, grad_gate, grad_up, grad_down)


def solution(mesh):
    return jax.shard_map(
        body,
        mesh=mesh,
        in_specs=(
            P(("dp", "expert"), None),
            P(("dp", "expert"), None),
            P(("dp", "expert"), None),
            P(("dp", "expert"), None),
            P("dp", None, None),
            P("dp", None, None),
            P("dp", None, None),
        ),
        out_specs=(
            P(("dp", "expert"), None),
            P(("dp", "expert"), None),
            P("dp", "expert", None),
            P("dp", "expert", None),
            P("dp", None, "expert"),
        ),
        check_vma=False,
    )
```

```python
import jax
import jax.numpy as jnp
from jax import lax
from jax.sharding import PartitionSpec as P


def expert_forward(arrived, w_gate, w_up, w_down):
    gate_act = jnp.einsum("erd,edf->erf", arrived, w_gate, preferred_element_type=jnp.float32)
    up_act = jnp.einsum("erd,edf->erf", arrived, w_up, preferred_element_type=jnp.float32)
    sigma_gate = jax.nn.sigmoid(gate_act)
    smooth = gate_act * sigma_gate
    hidden = (smooth * up_act).astype(jnp.bfloat16)
    result = jnp.einsum("erf,efd->erd", hidden, w_down, preferred_element_type=jnp.float32).astype(
        jnp.bfloat16
    )
    return (gate_act, up_act, sigma_gate, smooth, hidden, result)


def body(tokens, routes, gates, cotangent, w_gate, w_up, w_down):
    tok_rows, top_k = routes.shape
    width = tokens.shape[1]
    owners = lax.axis_size("dp")
    me = lax.axis_index("dp")
    per_owner = w_gate.shape[0]
    hidden_units = w_gate.shape[2]
    experts = owners * per_owner
    capacity = max(2, tok_rows * top_k * 5 // (4 * experts))
    rows_per_expert = owners * capacity
    side = jnp.zeros((tok_rows, 128 - 2 * top_k), jnp.bfloat16)
    both = jnp.concatenate(
        [tokens, cotangent, routes.astype(jnp.bfloat16), gates.astype(jnp.bfloat16), side], axis=1
    )
    all_both = lax.all_gather(both, "dp", axis=0, tiled=True)
    all_x = all_both[:, :width]
    all_c = all_both[:, width : 2 * width]
    all_routes = all_both[:, 2 * width : 2 * width + top_k].astype(jnp.int32)
    all_gates = all_both[:, 2 * width + top_k : 2 * width + 2 * top_k]
    mine = me * per_owner + jnp.arange(per_owner, dtype=jnp.int32)
    hit = all_routes[None, :, :] == mine[:, None, None]
    named = jnp.any(hit, axis=2).astype(jnp.int32)
    gain = jnp.sum(jnp.where(hit, all_gates[None, :, :].astype(jnp.float32), 0.0), axis=2)
    position = jnp.where(named > 0, jnp.cumsum(named, axis=1) - 1, -1)
    pick = position[:, None, :] == jnp.arange(rows_per_expert, dtype=jnp.int32)[None, :, None]
    pick_x = pick.astype(jnp.bfloat16)
    pick_g = jnp.where(pick, gain[:, None, :], 0.0).astype(jnp.bfloat16)
    arrived = jnp.einsum("ept,td->epd", pick_x, all_x, preferred_element_type=jnp.float32).astype(
        jnp.bfloat16
    )
    arrived_grad = jnp.einsum(
        "ept,td->epd", pick_g, all_c, preferred_element_type=jnp.float32
    ).astype(jnp.bfloat16)
    state = expert_forward(arrived, w_gate, w_up, w_down)
    gate_act, up_act, sigma_gate, smooth, hidden, result = state
    out_part = jnp.einsum("ept,epd->td", pick_g, result, preferred_element_type=jnp.float32).astype(
        jnp.bfloat16
    )
    layer_out = lax.psum_scatter(out_part, "dp", scatter_dimension=0, tiled=True)
    grad_hidden = jnp.einsum(
        "erd,efd->erf", arrived_grad, w_down, preferred_element_type=jnp.float32
    )
    grad_upact = (grad_hidden * smooth).astype(jnp.bfloat16)
    grad_gateact = (
        grad_hidden * up_act * sigma_gate * (1.0 + gate_act * (1.0 - sigma_gate))
    ).astype(jnp.bfloat16)
    row_grads = (
        jnp.einsum("erf,edf->erd", grad_gateact, w_gate, preferred_element_type=jnp.float32)
        + jnp.einsum("erf,edf->erd", grad_upact, w_up, preferred_element_type=jnp.float32)
    ).astype(jnp.bfloat16)
    grad_part = jnp.einsum(
        "ept,epd->td", pick_x, row_grads, preferred_element_type=jnp.float32
    ).astype(jnp.bfloat16)
    returned = lax.psum_scatter(
        jnp.concatenate([out_part, grad_part], axis=1), "dp", scatter_dimension=0, tiled=True
    )
    layer_out = returned[:, :width]
    grad_tokens = returned[:, width:]
    both_factors = jnp.concatenate([grad_gateact, grad_upact], axis=2)
    input_term = jnp.einsum(
        "erd,erf->def", arrived, both_factors, preferred_element_type=jnp.float32
    )
    down_term = jnp.einsum("erf,erd->def", hidden, arrived_grad, preferred_element_type=jnp.float32)
    totals = lax.psum_scatter(
        jnp.concatenate([input_term, down_term], axis=2).astype(jnp.bfloat16),
        "expert",
        scatter_dimension=0,
        tiled=True,
    ).astype(jnp.float32)
    grad_gate = jnp.transpose(totals[:, :, :hidden_units], (1, 0, 2)).astype(jnp.bfloat16)
    grad_up = jnp.transpose(totals[:, :, hidden_units : 2 * hidden_units], (1, 0, 2)).astype(
        jnp.bfloat16
    )
    grad_down = jnp.transpose(totals[:, :, 2 * hidden_units :], (1, 2, 0)).astype(jnp.bfloat16)
    return (layer_out, grad_tokens, grad_gate, grad_up, grad_down)


def solution(mesh):
    return jax.shard_map(
        body,
        mesh=mesh,
        in_specs=(
            P(("dp", "expert"), None),
            P(("dp", "expert"), None),
            P(("dp", "expert"), None),
            P(("dp", "expert"), None),
            P("dp", None, None),
            P("dp", None, None),
            P("dp", None, None),
        ),
        out_specs=(
            P(("dp", "expert"), None),
            P(("dp", "expert"), None),
            P("dp", "expert", None),
            P("dp", "expert", None),
            P("dp", None, "expert"),
        ),
        check_vma=False,
    )
```

```python
import jax
import jax.numpy as jnp
from jax import lax
from jax.sharding import PartitionSpec as P


def expert_forward(arrived, w_gate, w_up, w_down):
    gate_act = jnp.einsum("erd,edf->erf", arrived, w_gate, preferred_element_type=jnp.float32)
    up_act = jnp.einsum("erd,edf->erf", arrived, w_up, preferred_element_type=jnp.float32)
    sigma_gate = jax.nn.sigmoid(gate_act)
    smooth = gate_act * sigma_gate
    hidden = (smooth * up_act).astype(jnp.bfloat16)
    result = jnp.einsum("erf,efd->erd", hidden, w_down, preferred_element_type=jnp.float32).astype(
        jnp.bfloat16
    )
    return (gate_act, up_act, sigma_gate, smooth, hidden, result)


def body(tokens, routes, gates, cotangent, w_gate, w_up, w_down):
    tok_rows, top_k = routes.shape
    width = tokens.shape[1]
    owners = lax.axis_size("dp")
    me = lax.axis_index("dp")
    per_owner = w_gate.shape[0]
    hidden_units = w_gate.shape[2]
    experts = owners * per_owner
    capacity = max(2, tok_rows * top_k * 5 // (4 * experts))
    rows_per_expert = owners * capacity
    side = jnp.zeros((tok_rows, 128 - 2 * top_k), jnp.bfloat16)
    both = jnp.concatenate(
        [tokens, cotangent, routes.astype(jnp.bfloat16), gates.astype(jnp.bfloat16), side], axis=1
    )
    all_both = lax.all_gather(both, "dp", axis=0, tiled=True)
    all_x = all_both[:, :width]
    all_c = all_both[:, width : 2 * width]
    all_routes = all_both[:, 2 * width : 2 * width + top_k].astype(jnp.int32)
    all_gates = all_both[:, 2 * width + top_k : 2 * width + 2 * top_k]
    mine = me * per_owner + jnp.arange(per_owner, dtype=jnp.int32)
    hit = all_routes[None, :, :] == mine[:, None, None]
    named = jnp.any(hit, axis=2).astype(jnp.int32)
    gain = jnp.sum(jnp.where(hit, all_gates[None, :, :].astype(jnp.float32), 0.0), axis=2)
    position = jnp.where(named > 0, jnp.cumsum(named, axis=1) - 1, -1)
    pick = position[:, None, :] == jnp.arange(rows_per_expert, dtype=jnp.int32)[None, :, None]
    pick_x = pick.astype(jnp.bfloat16)
    pick_g = jnp.where(pick, gain[:, None, :], 0.0).astype(jnp.bfloat16)
    arrived = jnp.einsum("ept,td->epd", pick_x, all_x, preferred_element_type=jnp.float32).astype(
        jnp.bfloat16
    )
    arrived_grad = jnp.einsum(
        "ept,td->epd", pick_g, all_c, preferred_element_type=jnp.float32
    ).astype(jnp.bfloat16)
    state = expert_forward(arrived, w_gate, w_up, w_down)
    gate_act, up_act, sigma_gate, smooth, hidden, result = state
    out_part = jnp.einsum("ept,epd->td", pick_g, result, preferred_element_type=jnp.float32).astype(
        jnp.bfloat16
    )
    layer_out = lax.psum_scatter(out_part, "dp", scatter_dimension=0, tiled=True)
    grad_hidden = jnp.einsum(
        "erd,efd->erf", arrived_grad, w_down, preferred_element_type=jnp.float32
    )
    grad_upact = (grad_hidden * smooth).astype(jnp.bfloat16)
    grad_gateact = (
        grad_hidden * up_act * sigma_gate * (1.0 + gate_act * (1.0 - sigma_gate))
    ).astype(jnp.bfloat16)
    row_grads = (
        jnp.einsum("erf,edf->erd", grad_gateact, w_gate, preferred_element_type=jnp.float32)
        + jnp.einsum("erf,edf->erd", grad_upact, w_up, preferred_element_type=jnp.float32)
    ).astype(jnp.bfloat16)
    grad_part = jnp.einsum(
        "ept,epd->td", pick_x, row_grads, preferred_element_type=jnp.float32
    ).astype(jnp.bfloat16)
    grad_tokens = lax.psum_scatter(grad_part, "dp", scatter_dimension=0, tiled=True)
    both_factors = jnp.concatenate([grad_gateact, grad_upact], axis=2)
    input_term = jnp.einsum(
        "erd,erf->def", arrived, both_factors, preferred_element_type=jnp.float32
    )
    down_term = jnp.einsum("erf,erd->def", hidden, arrived_grad, preferred_element_type=jnp.float32)
    totals = lax.psum_scatter(
        jnp.concatenate([input_term, down_term], axis=2).astype(jnp.bfloat16),
        "expert",
        scatter_dimension=0,
        tiled=True,
    ).astype(jnp.float32)
    grad_gate = jnp.transpose(totals[:, :, :hidden_units], (1, 0, 2)).astype(jnp.bfloat16)
    grad_up = jnp.transpose(totals[:, :, hidden_units : 2 * hidden_units], (1, 0, 2)).astype(
        jnp.bfloat16
    )
    grad_down = jnp.transpose(totals[:, :, 2 * hidden_units :], (1, 2, 0)).astype(jnp.bfloat16)
    return (layer_out, grad_tokens, grad_gate, grad_up, grad_down)


def solution(mesh):
    return jax.shard_map(
        body,
        mesh=mesh,
        in_specs=(
            P(("dp", "expert"), None),
            P(("dp", "expert"), None),
            P(("dp", "expert"), None),
            P(("dp", "expert"), None),
            P("dp", None, None),
            P("dp", None, None),
            P("dp", None, None),
        ),
        out_specs=(
            P(("dp", "expert"), None),
            P(("dp", "expert"), None),
            P("dp", "expert", None),
            P("dp", "expert", None),
            P("dp", None, "expert"),
        ),
        check_vma=False,
    )
```
